32 devices in a mesh: groups: 2 (over y), seq: 4 (over z), segment: 2 (over x), owner: 2 (over core).
Axes of the slice: x: 2, y: 2, z: 4, core: 2. Of those that a mesh axis runs over, the one named last changes fastest.
Arguments:
- layer_input_rows: bfloat16 [2, 512, 5376], P('segment', ('groups', 'seq')), parts along dimension 1, may hold values from -40 to 40
- encoded_query_rows: bfloat16 [2, 512, 2048], P('segment', ('groups', 'seq'), 'owner'), parts along dimension 1, may hold values from -213 to 213
- encoded_key_rows: bfloat16 [2, 512, 1024], P('segment', ('groups', 'seq'), 'owner'), parts along dimension 1, may hold values from -6 to 6
- layer_norm_gain: float32 [2, 5376], P('segment'), may hold values from 0.25 to 1.75
- base_value_matrix: bfloat16 [2, 5376, 1024], P('segment', ('seq', 'owner')), may hold values from -0.078125 to 0.078125
- adapter_down_panels: bfloat16 [2, 8, 5376, 64], P('segment', 'seq', 'owner'), may hold values from -0.078125 to 0.078125
- adapter_up_panels: bfloat16 [2, 8, 64, 1024], P('segment', 'seq', None, 'owner'), may hold values from -0.75 to 0.75
- request_token_lengths: int32 [8], P('groups'), parts along dimension 0, may hold values from 1 to 128, 256 in all
- adapter_per_request: int32 [8], P('groups'), parts along dimension 0, may hold values from 0 to 7
- rank_per_adapter: int32 [8], replicated, may hold values from 16 to 64
- slot_per_adapter: int32 [8], replicated, may hold values from 0 to 7, each once
Outputs:
- layer_output: bfloat16 [2, 512, 2048], P('segment', ('groups', 'seq'), 'owner'), parts along dimension 1
The draws below stay inside these ranges and needn't reach their ends.
There are 2 independent parts, one for each index of `groups`. The reference program is written for one: setup_inputs(seed, part) draws one part's arguments, and reference() takes and returns one part's arrays. A program takes and returns all parts, laid end to end along the dimension named above; an argument that names none is the same for every part. Nothing has to cross between parts.
All inputs are finite; a program needn't handle non-finite values.
Results may differ from the reference program's by a relative error of at most 0.0065.
Values may be sent and summed in bfloat16 or wider, within the bound.
A program may use at most 128 MiB of HBM per device.

```python
import math
import jax
import jax.numpy as jnp
import numpy as np
from jax import lax

TOK_DEV = 64
MODEL_WIDTH = 5376
WINDOW = 1024
HEADS = 16
KEY_VALUE_HEADS = 8
HEAD_SIZE = 128
MAX_RANK = 64
REQUESTS = 4
LAYER_COUNT = 2
SLOT_COUNT = 8
TOKEN_COUNT = 256


def draw_layer_input_rows(key, part):
    first_key, second_key, third_key = jax.random.split(key, 3)
    column_scale = jnp.exp(jax.random.uniform(second_key, (1, 1, MODEL_WIDTH), jnp.float32, math.log(0.3), math.log(3.0)))
    row_scale = jnp.exp(jax.random.uniform(third_key, (LAYER_COUNT, TOKEN_COUNT, 1), jnp.float32, math.log(0.5), math.log(2.0)))
    drawn = jnp.clip(jax.random.normal(first_key, (LAYER_COUNT, TOKEN_COUNT, MODEL_WIDTH), jnp.float32), -6.0, 6.0)
    return (drawn * column_scale * row_scale).astype(jnp.bfloat16)


def attention_pair(key):
    folded = jax.random.fold_in(key, 11)
    draw_query, draw_keys = jax.random.split(folded, 2)
    group_size = HEADS // KEY_VALUE_HEADS
    key_draw = jnp.clip(jax.random.normal(draw_keys, (LAYER_COUNT, TOKEN_COUNT, KEY_VALUE_HEADS, HEAD_SIZE), jnp.float32), -6.0, 6.0)
    queries = jnp.clip(jax.random.normal(draw_query, (LAYER_COUNT, TOKEN_COUNT, KEY_VALUE_HEADS, group_size, HEAD_SIZE), jnp.float32), -6.0, 6.0)
    return (queries.reshape(LAYER_COUNT, TOKEN_COUNT, HEADS * HEAD_SIZE), key_draw.reshape(LAYER_COUNT, TOKEN_COUNT, KEY_VALUE_HEADS * HEAD_SIZE))


def draw_encoded_query_rows(key, part):
    return attention_pair(key)[0].astype(jnp.bfloat16)


def draw_encoded_key_rows(key, part):
    return attention_pair(key)[1].astype(jnp.bfloat16)


def set_ends(array, key, low, high):
    shape = array.shape
    spot = [jax.random.randint(jax.random.fold_in(key, axis), (), 0, shape[axis]) for axis in range(len(shape))]
    array = array.at[tuple(spot)].set(low)
    longest = shape.index(max(shape))
    spot[longest] = (spot[longest] + 1) % shape[longest]
    return array.at[tuple(spot)].set(high)


def level_of(key, dims, shards, low, high):
    factor_of = 1.0
    for axis_at, shards_of in shards:
        steps = jax.random.uniform(jax.random.fold_in(jax.random.fold_in(key, 6), axis_at), (shards_of,), jnp.float32, low / len(shards), high / len(shards))
        factor_of = factor_of * jnp.repeat(jnp.exp(steps), dims[axis_at] // shards_of).reshape((-1,) + (1,) * (len(dims) - 1 - axis_at))
    return factor_of


def length_profile(amount, total, reach, skew):
    weights = [(1 << 20) // math.isqrt(standing ** skew) + 1 for standing in range(2, amount + 1)]
    surplus, holding = total - reach - (amount - 1), [1] * (amount - 1)
    while surplus > 0:
        free = [i for i in range(amount - 1) if holding[i] < reach]
        pool, remaining = sum([weights[i] for i in free]), surplus
        for i in free:
            addition = min(reach - holding[i], max(1, remaining * weights[i] // pool), surplus)
            holding[i] = holding[i] + addition
            surplus = surplus - addition
    return np.array([reach] + holding)


def uneven_parts(rng, amount, total, limit, slope):
    if amount == 2:
        one = jax.random.randint(rng, (), max(1, total - limit), min(limit, total - 1) + 1)
        return jnp.stack([one, total - one])
    tallies = jnp.asarray(length_profile(amount, total, limit, slope), jnp.int32)
    twos = (amount - 1) // 2
    source_of, sink = tallies[1:1 + 2 * twos:2], tallies[2:2 + 2 * twos:2]
    margin = jnp.minimum(source_of - 1, limit - sink)
    moved = jax.random.randint(jax.random.fold_in(rng, 1), (twos,), 0, 1 << 20) % (margin + 1)
    tallies = tallies.at[1:1 + 2 * twos:2].set(source_of - moved).at[2:2 + 2 * twos:2].set(sink + moved)
    return tallies[jax.random.permutation(jax.random.fold_in(rng, 2), amount)]


def normal_values(rng, extent, deviation, bound, cuts=(), kind=jnp.bfloat16):
    array = deviation * jax.random.normal(rng, extent, jnp.float32)
    if cuts:
        array = array * level_of(rng, extent, cuts, -0.22, 0.18)
    return jnp.clip(array, -bound, bound).astype(kind)


def setup_inputs(seed: int = 0, part: int = 0) -> dict:
    arg_keys = jax.random.split(jax.random.key(seed), 12)
    own_keys = jax.random.split(jax.random.fold_in(arg_keys[11], part), 12)
    return {
        "layer_input_rows": draw_layer_input_rows(jax.random.fold_in(jax.random.fold_in(arg_keys[11], part), 71), part),
        "encoded_query_rows": draw_encoded_query_rows(jax.random.fold_in(jax.random.fold_in(arg_keys[11], part), 71), part),
        "encoded_key_rows": draw_encoded_key_rows(jax.random.fold_in(jax.random.fold_in(arg_keys[11], part), 71), part),
        "layer_norm_gain": jnp.clip(1.0 + 0.15 * jax.random.normal(arg_keys[3], (LAYER_COUNT, MODEL_WIDTH), jnp.float32), 0.25, 1.75),
        "base_value_matrix": normal_values(arg_keys[4], (LAYER_COUNT, MODEL_WIDTH, KEY_VALUE_HEADS * HEAD_SIZE), MODEL_WIDTH ** -0.5, 0.078125, ((0, 2), (1, 8))),
        "adapter_down_panels": normal_values(arg_keys[5], (LAYER_COUNT, SLOT_COUNT, MODEL_WIDTH, MAX_RANK), MODEL_WIDTH ** -0.5, 0.078125, ((0, 2), (1, 4), (2, 2))),
        "adapter_up_panels": normal_values(arg_keys[6], (LAYER_COUNT, SLOT_COUNT, MAX_RANK, KEY_VALUE_HEADS * HEAD_SIZE), MAX_RANK ** -0.5, 0.75, ((0, 2), (1, 4), (3, 2))),
        "request_token_lengths": uneven_parts(own_keys[7], REQUESTS, TOKEN_COUNT, TOKEN_COUNT // 2, 2).astype(jnp.int32),
        "adapter_per_request": set_ends(jax.random.randint(own_keys[8], (REQUESTS,), 0, SLOT_COUNT), jax.random.fold_in(own_keys[8], 1), 0, SLOT_COUNT - 1).astype(jnp.int32),
        "rank_per_adapter": set_ends(jax.random.randint(arg_keys[9], (SLOT_COUNT,), MAX_RANK // 4, MAX_RANK + 1), jax.random.fold_in(arg_keys[9], 1), MAX_RANK // 4, MAX_RANK).astype(jnp.int32),
        "slot_per_adapter": jax.random.permutation(arg_keys[10], SLOT_COUNT).astype(jnp.int32),
    }


query_scale = 168.0 ** (-0.5)
adapter_strength = 32.0
norm_eps = 1e-06

def requests_of(positions, request_token_lengths):
    request_ends = jnp.cumsum(request_token_lengths).astype(jnp.int32)
    return lax.optimization_barrier(jnp.sum((positions[:, None] >= request_ends[None, :]).astype(jnp.int32), axis=1))

def attend(queries, key_block_all, value_block_all, request_lookup):
    group_size = HEADS // KEY_VALUE_HEADS
    key_width = key_block_all.shape[1]
    keys_padded = jnp.concatenate([jnp.zeros((WINDOW, key_width), key_block_all.dtype), key_block_all], axis=0)
    values_padded = jnp.concatenate([jnp.zeros((WINDOW, key_width), value_block_all.dtype), value_block_all], axis=0)
    request_padded = jnp.concatenate([jnp.full((WINDOW,), -1, jnp.int32), request_lookup.astype(jnp.int32)], axis=0)
    key_span = WINDOW + TOK_DEV

    def one_block(block_index):
        first_row = (block_index * TOK_DEV).astype(jnp.int32)
        query_block = lax.dynamic_slice_in_dim(queries, first_row, TOK_DEV, 0).astype(jnp.float32)
        query_block = query_block.reshape(TOK_DEV, KEY_VALUE_HEADS, group_size, HEAD_SIZE)
        key_block = lax.dynamic_slice_in_dim(keys_padded, first_row, key_span, 0).astype(jnp.float32)
        key_block = key_block.reshape(key_span, KEY_VALUE_HEADS, HEAD_SIZE)
        value_block = lax.dynamic_slice_in_dim(values_padded, first_row, key_span, 0).astype(jnp.float32)
        value_block = value_block.reshape(key_span, KEY_VALUE_HEADS, HEAD_SIZE)
        own_requests = lax.dynamic_slice_in_dim(request_lookup.astype(jnp.int32), first_row, TOK_DEV, 0)
        seen_requests = lax.dynamic_slice_in_dim(request_padded, first_row, key_span, 0)
        query_place = first_row + jnp.arange(TOK_DEV, dtype=jnp.int32)
        key_place = first_row - WINDOW + jnp.arange(key_span, dtype=jnp.int32)
        live_mask = (key_place[None, :] <= query_place[:, None]) & (key_place[None, :] > query_place[:, None] - WINDOW)
        live_mask = live_mask & (seen_requests[None, :] == own_requests[:, None])
        scores = jnp.einsum('tgcd,jgd->gctj', query_block, key_block) * query_scale
        scores = jnp.where(live_mask[None, None], scores, jnp.float32(-1e+30))
        row_max = lax.optimization_barrier(jnp.max(scores, axis=-1, keepdims=True))
        weights = jnp.exp(scores - row_max)
        row_total = lax.optimization_barrier(jnp.sum(weights, axis=-1, keepdims=True))
        softmax_rows = (weights / row_total).astype(jnp.bfloat16)
        mixed_heads = jnp.einsum('gctj,jgd->tgcd', softmax_rows.astype(jnp.float32), value_block)
        return mixed_heads.astype(jnp.bfloat16).reshape(TOK_DEV, HEADS * HEAD_SIZE)
    blocks = lax.map(one_block, jnp.arange(TOKEN_COUNT // TOK_DEV, dtype=jnp.int32))
    return blocks.reshape(TOKEN_COUNT, HEADS * HEAD_SIZE)

def reference(layer_input_rows, encoded_query_rows, encoded_key_rows, layer_norm_gain, base_value_matrix, adapter_down_panels, adapter_up_panels, request_token_lengths, adapter_per_request, rank_per_adapter, slot_per_adapter):
    positions = jnp.arange(TOKEN_COUNT, dtype=jnp.int32)
    request_lookup = requests_of(positions, request_token_lengths)
    columns = jnp.arange(MAX_RANK, dtype=jnp.int32)
    outputs = []
    for layer_number in range(LAYER_COUNT):
        wide_rows = layer_input_rows[layer_number].astype(jnp.float32)
        normalized_rows = wide_rows * lax.rsqrt(lax.optimization_barrier(jnp.mean(wide_rows * wide_rows, axis=1, keepdims=True)) + norm_eps)
        normalized_rows = (normalized_rows * layer_norm_gain[layer_number][None, :]).astype(jnp.bfloat16)
        value_base_rows = jnp.dot(normalized_rows, base_value_matrix[layer_number], preferred_element_type=jnp.float32)
        reduced_rows = jnp.zeros((TOKEN_COUNT, MAX_RANK), jnp.float32)
        for request_number in range(REQUESTS):
            adapter_id = adapter_per_request[request_number]
            slot_number = slot_per_adapter[adapter_id]
            rank_value = rank_per_adapter[adapter_id]
            keep_mask = (request_lookup == request_number)[:, None] & (columns < rank_value)[None, :]
            matrix_product = jnp.dot(normalized_rows, adapter_down_panels[layer_number, slot_number], preferred_element_type=jnp.float32)
            reduced_rows = reduced_rows + jnp.where(keep_mask, matrix_product, jnp.float32(0.0))
        reduced_rows = reduced_rows.astype(jnp.bfloat16)
        adapter_value = jnp.zeros((TOKEN_COUNT, KEY_VALUE_HEADS * HEAD_SIZE), jnp.float32)
        for request_number in range(REQUESTS):
            adapter_id = adapter_per_request[request_number]
            slot_number = slot_per_adapter[adapter_id]
            adapter_scale = adapter_strength / rank_per_adapter[adapter_id].astype(jnp.float32)
            raised_rows = jnp.dot(reduced_rows, adapter_up_panels[layer_number, slot_number], preferred_element_type=jnp.float32)
            adapter_value = adapter_value + jnp.where((request_lookup == request_number)[:, None], adapter_scale * raised_rows, jnp.float32(0.0))
        value_output_rows = (value_base_rows + adapter_value).astype(jnp.bfloat16)
        outputs.append(attend(encoded_query_rows[layer_number], encoded_key_rows[layer_number], value_output_rows, request_lookup))
    return jnp.stack(outputs)
```

```python
import functools

import jax
import jax.numpy as jnp
from jax import lax
from jax.experimental import pallas as pl
from jax.experimental.pallas import tpu as pltpu
from jax.sharding import PartitionSpec as P

WINDOW = 1024
HEADS = 16
KEY_VALUE_HEADS = 8
HEAD_SIZE = 128


query_scale = 168.0 ** (-0.5)
adapter_strength = 32.0
norm_eps = 1e-06


def broadcast(x, axis, root):
    mine = lax.axis_index(axis) == root
    return lax.psum(jnp.where(mine, x, jnp.zeros_like(x)), axis)


def from_behind(value, axis, steps):
    count = lax.axis_size(axis)
    first, last = (max(0, -steps), min(count, count - steps))
    return lax.ppermute(value, axis, [(source, source + steps) for source in range(first, last)])


def per_device(
    layer_input_rows,
    encoded_query_rows,
    encoded_key_rows,
    layer_norm_gain,
    base_value_matrix,
    adapter_down_panels,
    adapter_up_panels,
    request_token_lengths,
    adapter_per_request,
    rank_per_adapter,
    slot_per_adapter,
):
    hidden = layer_input_rows[0]
    row_count = hidden.shape[0]
    seq_now = lax.axis_index("seq")
    owner_now = lax.axis_index("owner")
    reach_count = min(WINDOW // row_count, lax.axis_size("seq") - 1)
    requests = request_token_lengths.shape[0]
    library = slot_per_adapter.shape[0]
    slots_here = adapter_down_panels.shape[1]
    rows_halved = adapter_down_panels.shape[2]
    rank_span_width = adapter_down_panels.shape[3]
    key_value_halved = adapter_up_panels.shape[3]
    group_size = HEADS // KEY_VALUE_HEADS
    request_ends = jnp.cumsum(request_token_lengths)
    position = seq_now * row_count + jnp.arange(row_count, dtype=jnp.int32)
    context = seq_now * row_count + jnp.arange(-reach_count * row_count, row_count, dtype=jnp.int32)
    request_lookup = jnp.sum((position[:, None] >= request_ends[None, :]).astype(jnp.int32), axis=1)
    request_ctx = jnp.sum((context[:, None] >= request_ends[None, :]).astype(jnp.int32), axis=1)
    live_mask = (context[None, :] <= position[:, None]) & (
        context[None, :] > position[:, None] - WINDOW
    )
    live_mask = (
        live_mask & (context[None, :] >= 0) & (request_ctx[None, :] == request_lookup[:, None])
    )
    choose = adapter_per_request[:, None] == jnp.arange(library, dtype=jnp.int32)[None, :]
    slot_of = jnp.sum(jnp.where(choose, slot_per_adapter[None, :], 0), axis=1)
    rank_lookup = jnp.sum(jnp.where(choose, rank_per_adapter[None, :], 0), axis=1)
    scale_lookup = adapter_strength / rank_lookup.astype(jnp.float32)
    in_request = request_lookup[:, None] == jnp.arange(requests, dtype=jnp.int32)[None, :]
    column_live = jnp.arange(rank_span_width, dtype=jnp.int32)[None, :] < rank_lookup[:, None]
    row_gain_weight = jnp.where(in_request, scale_lookup[None, :], jnp.float32(0.0))
    down_panel_here = adapter_down_panels[0]
    up_panel_here = adapter_up_panels[0]
    queries = encoded_query_rows[0]
    keys_own = encoded_key_rows[0]
    key_heads = keys_own.shape[1] // HEAD_SIZE
    wide_rows = hidden.astype(jnp.float32)
    normalized_rows = wide_rows * lax.rsqrt(
        jnp.mean(wide_rows * wide_rows, axis=1, keepdims=True) + norm_eps
    )
    normalized_rows = (normalized_rows * layer_norm_gain[0][None, :]).astype(jnp.bfloat16)
    normed_half = lax.dynamic_slice_in_dim(normalized_rows, owner_now * rows_halved, rows_halved, 1)
    full_value = jnp.dot(
        normalized_rows,
        lax.all_gather(base_value_matrix[0], ("seq", "owner"), axis=0, tiled=True),
        preferred_element_type=jnp.float32,
    )
    value_base_rows = lax.dynamic_slice_in_dim(
        full_value, owner_now * key_value_halved, key_value_halved, 1
    )

    def fetch_one(reduced_rows, request_index):
        owner_slot = slot_of[request_index]
        holder = owner_slot // slots_here
        local_slot = owner_slot % slots_here
        down_local = lax.dynamic_slice_in_dim(down_panel_here, local_slot, 1, 0)
        up_local = lax.dynamic_slice_in_dim(up_panel_here, local_slot, 1, 0)
        down_piece, up_piece = (
            broadcast(down_local, "seq", holder),
            broadcast(up_local, "seq", holder),
        )
        keep_mask = in_request[:, request_index][:, None] & column_live[request_index][None, :]
        matrix_product = jnp.dot(normed_half, down_piece[0], preferred_element_type=jnp.float32)
        return (reduced_rows + jnp.where(keep_mask, matrix_product, jnp.float32(0.0)), up_piece[0])

    start_low = jnp.zeros((row_count, rank_span_width), jnp.float32)
    reduced_rows, panels_up = lax.scan(fetch_one, start_low, jnp.arange(requests, dtype=jnp.int32))
    reduced_rows = lax.psum(reduced_rows, "owner").astype(jnp.bfloat16)
    raised_rows = jnp.einsum(
        "tr,qrk->qtk", reduced_rows, panels_up, preferred_element_type=jnp.float32
    )
    adapter_value = jnp.sum(row_gain_weight.T[:, :, None] * raised_rows, axis=0)
    value_output_rows = (value_base_rows + adapter_value).astype(jnp.bfloat16)
    key_parts = []
    value_parts = []
    for shift_by in range(reach_count, 0, -1):
        key_piece, value_piece = from_behind((keys_own, value_output_rows), "seq", shift_by)
        key_parts.append(key_piece)
        value_parts.append(value_piece)
    keys_all = jnp.concatenate(key_parts + [keys_own], axis=0)
    values_all = jnp.concatenate(value_parts + [value_output_rows], axis=0)
    query_view = queries.reshape(row_count, key_heads, group_size, HEAD_SIZE)
    key_view = keys_all.reshape(-1, key_heads, HEAD_SIZE)
    value_view = values_all.reshape(-1, key_heads, HEAD_SIZE)
    head_outputs = []
    for head_index in range(key_heads):
        query_head = query_view[:, head_index]
        scores = (
            jnp.einsum(
                "tcd,jd->ctj",
                query_head,
                key_view[:, head_index],
                preferred_element_type=jnp.float32,
            )
            * query_scale
        )
        scores = jnp.where(live_mask[None], scores, jnp.float32(-1e30))
        row_max = jnp.max(scores, axis=-1, keepdims=True)
        weights = jnp.exp(scores - row_max)
        row_total = jnp.sum(weights, axis=-1, keepdims=True)
        softmax_rows = (weights / row_total).astype(jnp.bfloat16)
        mixed = jnp.einsum(
            "ctj,jd->tcd",
            softmax_rows,
            value_view[:, head_index],
            preferred_element_type=jnp.float32,
        )
        head_outputs.append(mixed.astype(jnp.bfloat16).reshape(row_count, group_size * HEAD_SIZE))
    result = jnp.concatenate(head_outputs, axis=1)
    return result[None]


ROWS, LANES = 16, 128


def kernel(
    n,
    lengths,
    adapters,
    ranks,
    slots,
    x_hbm,
    q_hbm,
    k_hbm,
    gain_hbm,
    w_hbm,
    down_hbm,
    up_hbm,
    out_hbm,
    xs,
    xf,
    gain,
    wbuf,
    dn,
    dcat,
    up,
    qb,
    kb,
    lp_mine,
    lp_other,
    part,
    vr,
    prob,
    ob,
    loc_sem,
    x_send_up,
    x_send_dn,
    x_recv,
    f_send,
    f_recv,
    w_send,
    w_recv,
    lp_send,
    lp_recv,
    q_send,
    q_recv,
    k_send,
    k_recv,
    rs_send,
    rs_recv,
    o_send,
    o_recv,
):
    f32, bf16 = jnp.float32, jnp.bfloat16
    s = lax.axis_index("seq")
    o = lax.axis_index("owner")
    tok, width = x_hbm.shape[1], x_hbm.shape[2]
    half = width // 2
    win = xf.shape[2]
    slab = w_hbm.shape[1]
    vcols = up.shape[2]
    panel_count, _, rank_width = dn.shape
    head_cols = vcols // n
    q_cols = qb.shape[2]
    group = HEADS // KEY_VALUE_HEADS
    requests = lengths.shape[0]
    total = n * tok
    chip_rows = width // n
    per_half = n // 2

    def window(of):
        inside = (of % per_half) * chip_rows
        first = min(inside // LANES * LANES, half - win)
        return first, inside - first

    c = s // per_half
    place = lax.rem(s, per_half)
    first, pad = 0, 0
    for step in range(per_half):
        a, b = window(step)
        first = jnp.where(place == step, a, first)
        pad = jnp.where(place == step, b, pad)
    first = pl.multiple_of(first, LANES)
    other = 1 - o

    def peer(seq, owner=None):
        return {"seq": seq, "owner": o if owner is None else owner}

    def remote(src, dst, send, recv, device):
        return pltpu.make_async_remote_copy(
            src_ref=src,
            dst_ref=dst,
            send_sem=send,
            recv_sem=recv,
            device_id=device,
            device_id_type=pl.DeviceIdType.MESH,
        )

    for step in range(per_half):
        _, b = window(step)

        @pl.when(place == step)
        def _():
            if b:
                wbuf[0:b, :] = jnp.zeros((b, vcols), bf16)
            rest = win - b - chip_rows
            if rest:
                wbuf[win - rest : win, :] = jnp.zeros((rest, vcols), bf16)

    barrier = pltpu.get_barrier_semaphore()
    for d in range(1, n):
        pl.semaphore_signal(
            barrier, inc=1, device_id=peer(lax.rem(s + d, n)), device_id_type=pl.DeviceIdType.MESH
        )
    pl.semaphore_signal(barrier, inc=1, device_id=peer(s, other), device_id_type=pl.DeviceIdType.MESH)

    w_at = pl.ds(pl.multiple_of(pad + o * slab, ROWS), slab)
    my_cols = pl.ds(pl.multiple_of(o * vcols, LANES), vcols)
    other_cols = pl.ds(pl.multiple_of(other * vcols, LANES), vcols)
    my_half = pl.ds(pl.multiple_of(o * half, LANES), half)
    x_window = pl.ds(pl.multiple_of(c * half + first, LANES), win)
    my_head = pl.ds(pl.multiple_of(s * head_cols, LANES), head_cols)
    my_q = pl.ds(pl.multiple_of(s * q_cols, LANES), q_cols)
    local = [
        pltpu.make_async_copy(x_hbm.at[0, :, my_half], xs.at[s], loc_sem.at[0]),
        pltpu.make_async_copy(x_hbm.at[0, :, x_window], xf.at[s], loc_sem.at[1]),
        pltpu.make_async_copy(gain_hbm, gain, loc_sem.at[2]),
        pltpu.make_async_copy(down_hbm.at[0], dn, loc_sem.at[3]),
        pltpu.make_async_copy(up_hbm.at[0], up, loc_sem.at[4]),
        pltpu.make_async_copy(w_hbm.at[0, :, my_cols], wbuf.at[w_at], loc_sem.at[5]),
        pltpu.make_async_copy(q_hbm.at[0, :, my_q], qb.at[s], loc_sem.at[6]),
        pltpu.make_async_copy(k_hbm.at[0, :, my_head], kb.at[s], loc_sem.at[7]),
    ]
    for copy in local:
        copy.start()

    pl.semaphore_wait(barrier, n)

    def x_copy(t, src, upward):
        to = s + 1 if upward else s - 1
        send = x_send_up if upward else x_send_dn
        return remote(src, xs.at[t], send.at[t], x_recv.at[t], peer(to))

    own_x = x_hbm.at[0, :, my_half]

    @pl.when(s < n - 1)
    def _():
        x_copy(s, own_x, True).start()

    @pl.when(s > 0)
    def _():
        x_copy(s, own_x, False).start()

    w_copy = remote(w_hbm.at[0, :, other_cols], wbuf.at[w_at], w_send, w_recv, peer(s, other))
    w_copy.start()

    def q_copy(to):
        cols = pl.ds(pl.multiple_of(to * q_cols, LANES), q_cols)
        return remote(q_hbm.at[0, :, cols], qb.at[s], q_send.at[to], q_recv.at[s], peer(to))

    def k_copy(to):
        cols = pl.ds(pl.multiple_of(to * head_cols, LANES), head_cols)
        return remote(k_hbm.at[0, :, cols], kb.at[s], k_send.at[to], k_recv.at[s], peer(to))

    for d in range(1, n):
        to = lax.rem(s + d, n)
        q_copy(to).start()
        k_copy(to).start()

    ends, slot_of, rank_of = [], [], []
    run = jnp.int32(0)
    for r in range(requests):
        run = run + lengths[r]
        ends.append(run)
        adapter = adapters[r]
        slot_of.append(slots[adapter])
        rank_of.append(ranks[adapter])

    def request_at(position):
        found = jnp.zeros(position.shape, jnp.int32)
        for r in range(requests):
            found = found + (position >= ends[r]).astype(jnp.int32)
        return found

    local[3].wait()
    for p in range(panel_count):
        dcat[:, p * rank_width : (p + 1) * rank_width] = dn[p]
    for at in (0, 1, 2, 4, 5):
        local[at].wait()

    def f_copy(t):
        return remote(
            xs.at[t, :, pl.ds(first, win)], xf.at[t], f_send.at[t], f_recv.at[t], peer(s, other)
        )

    def lp_copy(t):
        return remote(lp_mine.at[t], lp_other.at[t], lp_send.at[t], lp_recv.at[t], peer(s, other))

    def rs_copy(t, to):
        cols = pl.ds(pl.multiple_of(to * head_cols, LANES), head_cols)
        return remote(part.at[t, :, cols], vr.at[s, t], rs_send.at[t, to], rs_recv.at[s, t], peer(to))

    def low_part(t):
        rows = xs[t].astype(f32)
        scaled = (rows * gain[:, my_half]).astype(bf16)
        square = jnp.sum(rows * rows, axis=1, keepdims=True)
        product = jnp.dot(scaled, dcat[...], preferred_element_type=f32)
        lp_mine[t, :, : panel_count * rank_width] = product
        lp_mine[t, :, panel_count * rank_width :] = jnp.broadcast_to(square, (tok, LANES))
        lp_copy(t).start()

    def value_part(t):
        scaled = (xf[t].astype(f32) * gain[:, x_window]).astype(bf16)
        base = jnp.dot(scaled, wbuf[...], preferred_element_type=f32)
        lp_copy(t).wait_recv()
        low_width = panel_count * rank_width
        square = lp_mine[t, :, low_width : low_width + 1] + lp_other[t, :, low_width : low_width + 1]
        inv = lax.rsqrt(square / width + norm_eps)
        low = (lp_mine[t, :, :low_width] + lp_other[t, :, :low_width]) * inv
        req = request_at(t * tok + lax.broadcasted_iota(jnp.int32, (tok, 1), 0))
        slot_t = jnp.zeros((tok, 1), jnp.int32)
        rank_t = jnp.ones((tok, 1), jnp.int32)
        for r in range(requests):
            slot_t = jnp.where(req == r, slot_of[r], slot_t)
            rank_t = jnp.where(req == r, rank_of[r], rank_t)
        column = lax.broadcasted_iota(jnp.int32, (tok, low_width), 1)
        begin = (slot_t - s * panel_count) * rank_width
        low = jnp.where((column >= begin) & (column < begin + rank_t), low, 0.0).astype(bf16)
        raised = jnp.dot(low, up[...].reshape(low_width, vcols), preferred_element_type=f32)
        scale = adapter_strength / rank_t.astype(f32)
        part[t] = (base * inv + raised * scale).astype(bf16)
        for d in range(1, n):
            rs_copy(t, lax.rem(s + d, n)).start()
        vr[s, t] = part[t, :, my_head]

    low_part(s)
    w_copy.wait_recv()
    value_part(s)

    def attention():
        local[6].wait()
        local[7].wait()
        for d in range(1, n):
            frm = lax.rem(s + n - d, n)
            remote(qb.at[frm], qb.at[frm], q_send.at[frm], q_recv.at[frm], peer(frm)).wait_recv()
            remote(kb.at[frm], kb.at[frm], k_send.at[frm], k_recv.at[frm], peer(frm)).wait_recv()
        keys = kb[...].reshape(total, head_cols)
        key_at = lax.broadcasted_iota(jnp.int32, (1, total), 1)
        key_req = request_at(key_at)
        for t in range(n):
            query_at = t * tok + lax.broadcasted_iota(jnp.int32, (tok, 1), 0)
            live = (key_at <= query_at) & (key_at > query_at - WINDOW)
            live = live & (request_at(query_at) == key_req)
            for h in range(q_cols // HEAD_SIZE):
                query = qb[t, :, h * HEAD_SIZE : (h + 1) * HEAD_SIZE]
                kv = h // group
                scores = (
                    lax.dot_general(
                        query,
                        keys[:, kv * HEAD_SIZE : (kv + 1) * HEAD_SIZE],
                        (((1,), (1,)), ((), ())),
                        preferred_element_type=f32,
                    )
                    * query_scale
                )
                scores = jnp.where(live, scores, -1e30)
                weights = jnp.exp(scores - jnp.max(scores, axis=1, keepdims=True))
                soft = weights / jnp.sum(weights, axis=1, keepdims=True)
                prob[h, t * tok : (t + 1) * tok, :] = soft.astype(bf16)

    for d in range(1, n):
        if d == n - 1:
            attention()

        def arrive(below):
            t = s - d if below else s + d

            @pl.when((t >= 0) if below else (t < n))
            def _():
                x_copy(t, xs.at[t], below).wait_recv()

                @pl.when((s < n - 1) if below else (s > 0))
                def _():
                    x_copy(t, xs.at[t], below).start()

                @pl.when(o == c)
                def _():
                    f_copy(t).start()
                    xf[t] = xs[t, :, pl.ds(first, win)]

        arrive(True)
        arrive(False)

        def both(side, carry):
            t = s - d + 2 * d * side

            @pl.when((t >= 0) & (t < n))
            def _():
                low_part(t)

                @pl.when(o != c)
                def _():
                    f_copy(t).wait_recv()

                value_part(t)

            return carry

        lax.fori_loop(0, 2, both, 0)

    for d in range(1, n):
        frm = lax.rem(s + d, n)
        for t in range(n):
            remote(vr.at[frm, t], vr.at[frm, t], rs_send.at[t, frm], rs_recv.at[frm, t], peer(frm)).wait_recv()
    values = vr[0].astype(f32)
    for frm in range(1, n):
        values = values + vr[frm].astype(f32)
    values = values.reshape(total, head_cols).astype(bf16)

    def o_copy(t):
        return remote(ob.at[t], out_hbm.at[0, :, my_q], o_send.at[t], o_recv.at[s], peer(t))

    for h in range(q_cols // HEAD_SIZE):
        kv = h // group
        mixed = jnp.dot(
            prob[h], values[:, kv * HEAD_SIZE : (kv + 1) * HEAD_SIZE], preferred_element_type=f32
        ).astype(bf16)
        ob[:, :, h * HEAD_SIZE : (h + 1) * HEAD_SIZE] = mixed.reshape(n, tok, HEAD_SIZE)
    for d in range(1, n):
        o_copy(lax.rem(s + d, n)).start()
    mine = pltpu.make_async_copy(ob.at[s], out_hbm.at[0, :, my_q], loc_sem.at[8])
    mine.start()

    w_copy.wait_send()
    for d in range(1, n):
        to = lax.rem(s + d, n)
        q_copy(to).wait_send()
        k_copy(to).wait_send()
        for t in range(n):
            rs_copy(t, to).wait_send()
    for t in range(n):
        lp_copy(t).wait_send()

        @pl.when((t <= s) & (s < n - 1))
        def _():
            x_copy(t, xs.at[t], True).wait_send()

        @pl.when((t >= s) & (s > 0))
        def _():
            x_copy(t, xs.at[t], False).wait_send()

        @pl.when((o == c) & (t != s))
        def _():
            f_copy(t).wait_send()

    mine.wait()
    for d in range(1, n):
        frm = lax.rem(s + d, n)
        o_copy(frm).wait_send()
        cols = pl.ds(pl.multiple_of(frm * q_cols, LANES), q_cols)
        remote(ob.at[frm], out_hbm.at[0, :, cols], o_send.at[frm], o_recv.at[frm], peer(frm)).wait_recv()


def fused(
    n,
    layer_input_rows,
    encoded_query_rows,
    encoded_key_rows,
    layer_norm_gain,
    base_value_matrix,
    adapter_down_panels,
    adapter_up_panels,
    request_token_lengths,
    adapter_per_request,
    rank_per_adapter,
    slot_per_adapter,
):
    f32, bf16 = jnp.float32, jnp.bfloat16
    tok, width = layer_input_rows.shape[1:]
    half = width // 2
    panels, _, rank_width = adapter_down_panels.shape[1:]
    vcols = adapter_up_panels.shape[3]
    qcols = encoded_query_rows.shape[2]
    chip_rows = width // n
    pads = [(i * chip_rows) % LANES for i in range(n // 2)]
    win = -(-(max(pads) + chip_rows) // LANES) * LANES
    total = n * tok
    low = panels * rank_width
    dma = pltpu.SemaphoreType.DMA
    any_spec = pl.BlockSpec(memory_space=pl.ANY)
    smem = pl.BlockSpec(memory_space=pltpu.SMEM)
    return pl.pallas_call(
        functools.partial(kernel, n),
        out_shape=jax.ShapeDtypeStruct(encoded_query_rows.shape, bf16),
        in_specs=[smem] * 4 + [any_spec] * 7,
        out_specs=any_spec,
        scratch_shapes=[
            pltpu.VMEM((n, tok, half), bf16),
            pltpu.VMEM((n, tok, win), bf16),
            pltpu.VMEM((1, width), f32),
            pltpu.VMEM((win, vcols), bf16),
            pltpu.VMEM((panels, half, rank_width), bf16),
            pltpu.VMEM((half, low), bf16),
            pltpu.VMEM((panels, rank_width, vcols), bf16),
            pltpu.VMEM((n, tok, qcols // n), bf16),
            pltpu.VMEM((n, tok, vcols // n), bf16),
            pltpu.VMEM((n, tok, low + LANES), f32),
            pltpu.VMEM((n, tok, low + LANES), f32),
            pltpu.VMEM((n, tok, vcols), bf16),
            pltpu.VMEM((n, n, tok, vcols // n), bf16),
            pltpu.VMEM((qcols // n // HEAD_SIZE, total, total), bf16),
            pltpu.VMEM((n, tok, qcols // n), bf16),
            dma((9,)),
            dma((n,)),
            dma((n,)),
            dma((n,)),
            dma((n,)),
            dma((n,)),
            dma,
            dma,
            dma((n,)),
            dma((n,)),
            dma((n,)),
            dma((n,)),
            dma((n,)),
            dma((n,)),
            dma((n, n)),
            dma((n, n)),
            dma((n,)),
            dma((n,)),
        ],
        compiler_params=pltpu.CompilerParams(
            collective_id=0, has_side_effects=True, vmem_limit_bytes=56 * 1024 * 1024
        ),
    )(
        request_token_lengths,
        adapter_per_request,
        rank_per_adapter,
        slot_per_adapter,
        layer_input_rows,
        encoded_query_rows,
        encoded_key_rows,
        layer_norm_gain,
        base_value_matrix,
        adapter_down_panels,
        adapter_up_panels,
    )


def solution(mesh):
    in_specs = (
        P("segment", ("groups", "seq"), None),
        P("segment", ("groups", "seq"), "owner"),
        P("segment", ("groups", "seq"), "owner"),
        P("segment", None),
        P("segment", ("seq", "owner"), None),
        P("segment", "seq", "owner", None),
        P("segment", "seq", None, "owner"),
        P("groups"),
        P("groups"),
        P(),
        P(),
    )
    out_specs = P("segment", ("groups", "seq"), "owner")
    n = mesh.shape["seq"]
    key_heads = KEY_VALUE_HEADS // mesh.shape["owner"]
    small = mesh.shape["owner"] == 2 and n % 2 == 0 and key_heads % n == 0
    return jax.shard_map(
        functools.partial(fused, n) if small else per_device, mesh=mesh, in_specs=in_specs, out_specs=out_specs, check_vma=False
    )
```

```python
import functools

import jax
import jax.numpy as jnp
from jax import lax
from jax.experimental import pallas as pl
from jax.experimental.pallas import tpu as pltpu
from jax.sharding import PartitionSpec as P

WINDOW = 1024
HEADS = 16
KEY_VALUE_HEADS = 8
HEAD_SIZE = 128


query_scale = 168.0 ** (-0.5)
adapter_strength = 32.0
norm_eps = 1e-06


def broadcast(x, axis, root):
    mine = lax.axis_index(axis) == root
    return lax.psum(jnp.where(mine, x, jnp.zeros_like(x)), axis)


def from_behind(value, axis, steps):
    count = lax.axis_size(axis)
    first, last = (max(0, -steps), min(count, count - steps))
    return lax.ppermute(value, axis, [(source, source + steps) for source in range(first, last)])


def per_device(
    layer_input_rows,
    encoded_query_rows,
    encoded_key_rows,
    layer_norm_gain,
    base_value_matrix,
    adapter_down_panels,
    adapter_up_panels,
    request_token_lengths,
    adapter_per_request,
    rank_per_adapter,
    slot_per_adapter,
):
    hidden = layer_input_rows[0]
    row_count = hidden.shape[0]
    seq_now = lax.axis_index("seq")
    owner_now = lax.axis_index("owner")
    reach_count = min(WINDOW // row_count, lax.axis_size("seq") - 1)
    requests = request_token_lengths.shape[0]
    library = slot_per_adapter.shape[0]
    slots_here = adapter_down_panels.shape[1]
    rows_halved = adapter_down_panels.shape[2]
    rank_span_width = adapter_down_panels.shape[3]
    key_value_halved = adapter_up_panels.shape[3]
    group_size = HEADS // KEY_VALUE_HEADS
    request_ends = jnp.cumsum(request_token_lengths)
    position = seq_now * row_count + jnp.arange(row_count, dtype=jnp.int32)
    context = seq_now * row_count + jnp.arange(-reach_count * row_count, row_count, dtype=jnp.int32)
    request_lookup = jnp.sum((position[:, None] >= request_ends[None, :]).astype(jnp.int32), axis=1)
    request_ctx = jnp.sum((context[:, None] >= request_ends[None, :]).astype(jnp.int32), axis=1)
    live_mask = (context[None, :] <= position[:, None]) & (
        context[None, :] > position[:, None] - WINDOW
    )
    live_mask = (
        live_mask & (context[None, :] >= 0) & (request_ctx[None, :] == request_lookup[:, None])
    )
    choose = adapter_per_request[:, None] == jnp.arange(library, dtype=jnp.int32)[None, :]
    slot_of = jnp.sum(jnp.where(choose, slot_per_adapter[None, :], 0), axis=1)
    rank_lookup = jnp.sum(jnp.where(choose, rank_per_adapter[None, :], 0), axis=1)
    scale_lookup = adapter_strength / rank_lookup.astype(jnp.float32)
    in_request = request_lookup[:, None] == jnp.arange(requests, dtype=jnp.int32)[None, :]
    column_live = jnp.arange(rank_span_width, dtype=jnp.int32)[None, :] < rank_lookup[:, None]
    row_gain_weight = jnp.where(in_request, scale_lookup[None, :], jnp.float32(0.0))
    down_panel_here = adapter_down_panels[0]
    up_panel_here = adapter_up_panels[0]
    queries = encoded_query_rows[0]
    keys_own = encoded_key_rows[0]
    key_heads = keys_own.shape[1] // HEAD_SIZE
    wide_rows = hidden.astype(jnp.float32)
    normalized_rows = wide_rows * lax.rsqrt(
        jnp.mean(wide_rows * wide_rows, axis=1, keepdims=True) + norm_eps
    )
    normalized_rows = (normalized_rows * layer_norm_gain[0][None, :]).astype(jnp.bfloat16)
    normed_half = lax.dynamic_slice_in_dim(normalized_rows, owner_now * rows_halved, rows_halved, 1)
    full_value = jnp.dot(
        normalized_rows,
        lax.all_gather(base_value_matrix[0], ("seq", "owner"), axis=0, tiled=True),
        preferred_element_type=jnp.float32,
    )
    value_base_rows = lax.dynamic_slice_in_dim(
        full_value, owner_now * key_value_halved, key_value_halved, 1
    )

    def fetch_one(reduced_rows, request_index):
        owner_slot = slot_of[request_index]
        holder = owner_slot // slots_here
        local_slot = owner_slot % slots_here
        down_local = lax.dynamic_slice_in_dim(down_panel_here, local_slot, 1, 0)
        up_local = lax.dynamic_slice_in_dim(up_panel_here, local_slot, 1, 0)
        down_piece, up_piece = (
            broadcast(down_local, "seq", holder),
            broadcast(up_local, "seq", holder),
        )
        keep_mask = in_request[:, request_index][:, None] & column_live[request_index][None, :]
        matrix_product = jnp.dot(normed_half, down_piece[0], preferred_element_type=jnp.float32)
        return (reduced_rows + jnp.where(keep_mask, matrix_product, jnp.float32(0.0)), up_piece[0])

    start_low = jnp.zeros((row_count, rank_span_width), jnp.float32)
    reduced_rows, panels_up = lax.scan(fetch_one, start_low, jnp.arange(requests, dtype=jnp.int32))
    reduced_rows = lax.psum(reduced_rows, "owner").astype(jnp.bfloat16)
    raised_rows = jnp.einsum(
        "tr,qrk->qtk", reduced_rows, panels_up, preferred_element_type=jnp.float32
    )
    adapter_value = jnp.sum(row_gain_weight.T[:, :, None] * raised_rows, axis=0)
    value_output_rows = (value_base_rows + adapter_value).astype(jnp.bfloat16)
    key_parts = []
    value_parts = []
    for shift_by in range(reach_count, 0, -1):
        key_piece, value_piece = from_behind((keys_own, value_output_rows), "seq", shift_by)
        key_parts.append(key_piece)
        value_parts.append(value_piece)
    keys_all = jnp.concatenate(key_parts + [keys_own], axis=0)
    values_all = jnp.concatenate(value_parts + [value_output_rows], axis=0)
    query_view = queries.reshape(row_count, key_heads, group_size, HEAD_SIZE)
    key_view = keys_all.reshape(-1, key_heads, HEAD_SIZE)
    value_view = values_all.reshape(-1, key_heads, HEAD_SIZE)
    head_outputs = []
    for head_index in range(key_heads):
        query_head = query_view[:, head_index]
        scores = (
            jnp.einsum(
                "tcd,jd->ctj",
                query_head,
                key_view[:, head_index],
                preferred_element_type=jnp.float32,
            )
            * query_scale
        )
        scores = jnp.where(live_mask[None], scores, jnp.float32(-1e30))
        row_max = jnp.max(scores, axis=-1, keepdims=True)
        weights = jnp.exp(scores - row_max)
        row_total = jnp.sum(weights, axis=-1, keepdims=True)
        softmax_rows = (weights / row_total).astype(jnp.bfloat16)
        mixed = jnp.einsum(
            "ctj,jd->tcd",
            softmax_rows,
            value_view[:, head_index],
            preferred_element_type=jnp.float32,
        )
        head_outputs.append(mixed.astype(jnp.bfloat16).reshape(row_count, group_size * HEAD_SIZE))
    result = jnp.concatenate(head_outputs, axis=1)
    return result[None]


ROWS, LANES = 16, 128


def kernel(
    n,
    lengths,
    adapters,
    ranks,
    slots,
    x_hbm,
    q_hbm,
    k_hbm,
    gain_hbm,
    w_hbm,
    down_hbm,
    up_hbm,
    out_hbm,
    xs,
    xf,
    gain,
    wbuf,
    dn,
    up,
    qb,
    kb,
    lp_mine,
    lp_other,
    part,
    vr,
    prob,
    ob,
    loc_sem,
    x_send_up,
    x_send_dn,
    x_recv,
    f_send,
    f_recv,
    w_send,
    w_recv,
    lp_send,
    lp_recv,
    q_send,
    q_recv,
    k_send,
    k_recv,
    rs_send,
    rs_recv,
    o_send,
    o_recv,
):
    f32, bf16 = jnp.float32, jnp.bfloat16
    s = lax.axis_index("seq")
    o = lax.axis_index("owner")
    tok, width = x_hbm.shape[1], x_hbm.shape[2]
    half = width // 2
    win = xf.shape[2]
    slab = w_hbm.shape[1]
    vcols = up.shape[2]
    panel_count, rank_width, _ = dn.shape
    head_cols = vcols // n
    q_cols = qb.shape[2]
    group = HEADS // KEY_VALUE_HEADS
    requests = lengths.shape[0]
    total = n * tok
    chip_rows = width // n
    per_half = n // 2

    def window(of):
        inside = (of % per_half) * chip_rows
        first = min(inside // LANES * LANES, half - win)
        return first, inside - first

    c = s // per_half
    place = lax.rem(s, per_half)
    first, pad = 0, 0
    for step in range(per_half):
        a, b = window(step)
        first = jnp.where(place == step, a, first)
        pad = jnp.where(place == step, b, pad)
    first = pl.multiple_of(first, LANES)
    other = 1 - o

    def peer(seq, owner=None):
        return {"seq": seq, "owner": o if owner is None else owner}

    def remote(src, dst, send, recv, device):
        return pltpu.make_async_remote_copy(
            src_ref=src,
            dst_ref=dst,
            send_sem=send,
            recv_sem=recv,
            device_id=device,
            device_id_type=pl.DeviceIdType.MESH,
        )

    for step in range(per_half):
        _, b = window(step)

        @pl.when(place == step)
        def _():
            if b:
                wbuf[0:b, :] = jnp.zeros((b, vcols), bf16)
            rest = win - b - chip_rows
            if rest:
                wbuf[win - rest : win, :] = jnp.zeros((rest, vcols), bf16)

    barrier = pltpu.get_barrier_semaphore()
    for d in range(1, n):
        pl.semaphore_signal(
            barrier, inc=1, device_id=peer(lax.rem(s + d, n)), device_id_type=pl.DeviceIdType.MESH
        )
    pl.semaphore_signal(barrier, inc=1, device_id=peer(s, other), device_id_type=pl.DeviceIdType.MESH)

    w_at = pl.ds(pl.multiple_of(pad + o * slab, ROWS), slab)
    my_cols = pl.ds(pl.multiple_of(o * vcols, LANES), vcols)
    other_cols = pl.ds(pl.multiple_of(other * vcols, LANES), vcols)
    my_half = pl.ds(pl.multiple_of(o * half, LANES), half)
    x_window = pl.ds(pl.multiple_of(c * half + first, LANES), win)
    my_head = pl.ds(pl.multiple_of(s * head_cols, LANES), head_cols)
    my_q = pl.ds(pl.multiple_of(s * q_cols, LANES), q_cols)
    local = [
        pltpu.make_async_copy(x_hbm.at[0, :, my_half], xs.at[s], loc_sem.at[0]),
        pltpu.make_async_copy(x_hbm.at[0, :, x_window], xf.at[s], loc_sem.at[1]),
        pltpu.make_async_copy(gain_hbm, gain, loc_sem.at[2]),
        pltpu.make_async_copy(down_hbm.at[0], dn, loc_sem.at[3]),
        pltpu.make_async_copy(up_hbm.at[0], up, loc_sem.at[4]),
        pltpu.make_async_copy(w_hbm.at[0, :, my_cols], wbuf.at[w_at], loc_sem.at[5]),
        pltpu.make_async_copy(q_hbm.at[0, :, my_q], qb.at[s], loc_sem.at[6]),
        pltpu.make_async_copy(k_hbm.at[0, :, my_head], kb.at[s], loc_sem.at[7]),
    ]
    for copy in local:
        copy.start()

    pl.semaphore_wait(barrier, n)

    def x_copy(t, src, upward):
        to = s + 1 if upward else s - 1
        send = x_send_up if upward else x_send_dn
        return remote(src, xs.at[t], send.at[t], x_recv.at[t], peer(to))

    own_x = x_hbm.at[0, :, my_half]

    @pl.when(s < n - 1)
    def _():
        x_copy(s, own_x, True).start()

    @pl.when(s > 0)
    def _():
        x_copy(s, own_x, False).start()

    w_copy = remote(w_hbm.at[0, :, other_cols], wbuf.at[w_at], w_send, w_recv, peer(s, other))
    w_copy.start()

    def q_copy(to):
        cols = pl.ds(pl.multiple_of(to * q_cols, LANES), q_cols)
        return remote(q_hbm.at[0, :, cols], qb.at[s], q_send.at[to], q_recv.at[s], peer(to))

    def k_copy(to):
        cols = pl.ds(pl.multiple_of(to * head_cols, LANES), head_cols)
        return remote(k_hbm.at[0, :, cols], kb.at[s], k_send.at[to], k_recv.at[s], peer(to))

    for d in range(1, n):
        to = lax.rem(s + d, n)
        q_copy(to).start()
        k_copy(to).start()

    ends, slot_of, rank_of = [], [], []
    run = jnp.int32(0)
    for r in range(requests):
        run = run + lengths[r]
        ends.append(run)
        adapter = adapters[r]
        slot_of.append(slots[adapter])
        rank_of.append(ranks[adapter])

    def request_at(position):
        found = jnp.zeros(position.shape, jnp.int32)
        for r in range(requests):
            found = found + (position >= ends[r]).astype(jnp.int32)
        return found

    for at in range(6):
        local[at].wait()

    def f_copy(t):
        return remote(
            xs.at[t, :, pl.ds(first, win)], xf.at[t], f_send.at[t], f_recv.at[t], peer(s, other)
        )

    def lp_copy(t):
        return remote(lp_mine.at[t], lp_other.at[t], lp_send.at[t], lp_recv.at[t], peer(s, other))

    def rs_copy(t, to):
        cols = pl.ds(pl.multiple_of(to * head_cols, LANES), head_cols)
        return remote(part.at[t, :, cols], vr.at[s, t], rs_send.at[t, to], rs_recv.at[s, t], peer(to))

    def low_part(t):
        rows = xs[t].astype(f32)
        scaled = (rows * gain[:, my_half]).astype(bf16)
        square = jnp.sum(rows * rows, axis=1, keepdims=True)
        product = lax.dot_general(
            scaled,
            dn[...].reshape(panel_count * rank_width, half),
            (((1,), (1,)), ((), ())),
            preferred_element_type=f32,
        )
        lp_mine[t, :, : panel_count * rank_width] = product
        lp_mine[t, :, panel_count * rank_width :] = jnp.broadcast_to(square, (tok, LANES))
        lp_copy(t).start()

    def value_part(t):
        scaled = (xf[t].astype(f32) * gain[:, x_window]).astype(bf16)
        base = jnp.dot(scaled, wbuf[...], preferred_element_type=f32)
        lp_copy(t).wait_recv()
        low_width = panel_count * rank_width
        square = lp_mine[t, :, low_width : low_width + 1] + lp_other[t, :, low_width : low_width + 1]
        inv = lax.rsqrt(square / width + norm_eps)
        low = (lp_mine[t, :, :low_width] + lp_other[t, :, :low_width]) * inv
        req = request_at(t * tok + lax.broadcasted_iota(jnp.int32, (tok, 1), 0))
        slot_t = jnp.zeros((tok, 1), jnp.int32)
        rank_t = jnp.ones((tok, 1), jnp.int32)
        for r in range(requests):
            slot_t = jnp.where(req == r, slot_of[r], slot_t)
            rank_t = jnp.where(req == r, rank_of[r], rank_t)
        column = lax.broadcasted_iota(jnp.int32, (tok, low_width), 1)
        begin = (slot_t - s * panel_count) * rank_width
        low = jnp.where((column >= begin) & (column < begin + rank_t), low, 0.0).astype(bf16)
        raised = jnp.dot(low, up[...].reshape(low_width, vcols), preferred_element_type=f32)
        scale = adapter_strength / rank_t.astype(f32)
        part[t] = (base * inv + raised * scale).astype(bf16)
        for d in range(1, n):
            rs_copy(t, lax.rem(s + d, n)).start()
        vr[s, t] = part[t, :, my_head]

    low_part(s)

    def attention():
        local[6].wait()
        local[7].wait()
        for d in range(1, n):
            frm = lax.rem(s + n - d, n)
            remote(qb.at[frm], qb.at[frm], q_send.at[frm], q_recv.at[frm], peer(frm)).wait_recv()
            remote(kb.at[frm], kb.at[frm], k_send.at[frm], k_recv.at[frm], peer(frm)).wait_recv()
        keys = kb[...].reshape(total, head_cols)
        key_at = lax.broadcasted_iota(jnp.int32, (1, total), 1)
        key_req = request_at(key_at)
        for t in range(n):
            query_at = t * tok + lax.broadcasted_iota(jnp.int32, (tok, 1), 0)
            live = (key_at <= query_at) & (key_at > query_at - WINDOW)
            live = live & (request_at(query_at) == key_req)
            for h in range(q_cols // HEAD_SIZE):
                query = qb[t, :, h * HEAD_SIZE : (h + 1) * HEAD_SIZE]
                kv = h // group
                scores = (
                    lax.dot_general(
                        query,
                        keys[:, kv * HEAD_SIZE : (kv + 1) * HEAD_SIZE],
                        (((1,), (1,)), ((), ())),
                        preferred_element_type=f32,
                    )
                    * query_scale
                )
                scores = jnp.where(live, scores, -1e30)
                weights = jnp.exp(scores - jnp.max(scores, axis=1, keepdims=True))
                soft = weights / jnp.sum(weights, axis=1, keepdims=True)
                prob[h, t * tok : (t + 1) * tok, :] = soft.astype(bf16)

    for d in range(1, n):
        if d == n - 1:
            attention()

        def arrive(below):
            t = s - d if below else s + d

            @pl.when((t >= 0) if below else (t < n))
            def _():
                x_copy(t, xs.at[t], below).wait_recv()

                @pl.when((s < n - 1) if below else (s > 0))
                def _():
                    x_copy(t, xs.at[t], below).start()

                @pl.when(o == c)
                def _():
                    f_copy(t).start()
                    xf[t] = xs[t, :, pl.ds(first, win)]

        arrive(True)
        arrive(False)

        if d == 1:
            w_copy.wait_recv()
            value_part(s)

        def both(side, carry):
            t = s - d + 2 * d * side

            @pl.when((t >= 0) & (t < n))
            def _():
                low_part(t)

                @pl.when(o != c)
                def _():
                    f_copy(t).wait_recv()

                value_part(t)

            return carry

        lax.fori_loop(0, 2, both, 0)

    for d in range(1, n):
        frm = lax.rem(s + d, n)
        for t in range(n):
            remote(vr.at[frm, t], vr.at[frm, t], rs_send.at[t, frm], rs_recv.at[frm, t], peer(frm)).wait_recv()
    values = vr[0].astype(f32)
    for frm in range(1, n):
        values = values + vr[frm].astype(f32)
    values = values.reshape(total, head_cols).astype(bf16)

    def o_copy(t):
        return remote(ob.at[t], out_hbm.at[0, :, my_q], o_send.at[t], o_recv.at[s], peer(t))

    for h in range(q_cols // HEAD_SIZE):
        kv = h // group
        mixed = jnp.dot(
            prob[h], values[:, kv * HEAD_SIZE : (kv + 1) * HEAD_SIZE], preferred_element_type=f32
        ).astype(bf16)
        ob[:, :, h * HEAD_SIZE : (h + 1) * HEAD_SIZE] = mixed.reshape(n, tok, HEAD_SIZE)
    for d in range(1, n):
        o_copy(lax.rem(s + d, n)).start()
    mine = pltpu.make_async_copy(ob.at[s], out_hbm.at[0, :, my_q], loc_sem.at[8])
    mine.start()

    w_copy.wait_send()
    for d in range(1, n):
        to = lax.rem(s + d, n)
        q_copy(to).wait_send()
        k_copy(to).wait_send()
        for t in range(n):
            rs_copy(t, to).wait_send()
    for t in range(n):
        lp_copy(t).wait_send()

        @pl.when((t <= s) & (s < n - 1))
        def _():
            x_copy(t, xs.at[t], True).wait_send()

        @pl.when((t >= s) & (s > 0))
        def _():
            x_copy(t, xs.at[t], False).wait_send()

        @pl.when((o == c) & (t != s))
        def _():
            f_copy(t).wait_send()

    mine.wait()
    for d in range(1, n):
        frm = lax.rem(s + d, n)
        o_copy(frm).wait_send()
        cols = pl.ds(pl.multiple_of(frm * q_cols, LANES), q_cols)
        remote(ob.at[frm], out_hbm.at[0, :, cols], o_send.at[frm], o_recv.at[frm], peer(frm)).wait_recv()


def fused(
    n,
    layer_input_rows,
    encoded_query_rows,
    encoded_key_rows,
    layer_norm_gain,
    base_value_matrix,
    adapter_down_panels,
    adapter_up_panels,
    request_token_lengths,
    adapter_per_request,
    rank_per_adapter,
    slot_per_adapter,
):
    f32, bf16 = jnp.float32, jnp.bfloat16
    tok, width = layer_input_rows.shape[1:]
    half = width // 2
    panels, _, rank_width = adapter_down_panels.shape[1:]
    vcols = adapter_up_panels.shape[3]
    qcols = encoded_query_rows.shape[2]
    chip_rows = width // n
    pads = [(i * chip_rows) % LANES for i in range(n // 2)]
    win = -(-(max(pads) + chip_rows) // LANES) * LANES
    total = n * tok
    low = panels * rank_width
    dma = pltpu.SemaphoreType.DMA
    any_spec = pl.BlockSpec(memory_space=pl.ANY)
    smem = pl.BlockSpec(memory_space=pltpu.SMEM)
    return pl.pallas_call(
        functools.partial(kernel, n),
        out_shape=jax.ShapeDtypeStruct(encoded_query_rows.shape, bf16),
        in_specs=[smem] * 4 + [any_spec] * 7,
        out_specs=any_spec,
        scratch_shapes=[
            pltpu.VMEM((n, tok, half), bf16),
            pltpu.VMEM((n, tok, win), bf16),
            pltpu.VMEM((1, width), f32),
            pltpu.VMEM((win, vcols), bf16),
            pltpu.VMEM((panels, rank_width, half), bf16),
            pltpu.VMEM((panels, rank_width, vcols), bf16),
            pltpu.VMEM((n, tok, qcols // n), bf16),
            pltpu.VMEM((n, tok, vcols // n), bf16),
            pltpu.VMEM((n, tok, low + LANES), f32),
            pltpu.VMEM((n, tok, low + LANES), f32),
            pltpu.VMEM((n, tok, vcols), bf16),
            pltpu.VMEM((n, n, tok, vcols // n), bf16),
            pltpu.VMEM((qcols // n // HEAD_SIZE, total, total), bf16),
            pltpu.VMEM((n, tok, qcols // n), bf16),
            dma((9,)),
            dma((n,)),
            dma((n,)),
            dma((n,)),
            dma((n,)),
            dma((n,)),
            dma,
            dma,
            dma((n,)),
            dma((n,)),
            dma((n,)),
            dma((n,)),
            dma((n,)),
            dma((n,)),
            dma((n, n)),
            dma((n, n)),
            dma((n,)),
            dma((n,)),
        ],
        compiler_params=pltpu.CompilerParams(
            collective_id=0, has_side_effects=True, vmem_limit_bytes=56 * 1024 * 1024
        ),
    )(
        request_token_lengths,
        adapter_per_request,
        rank_per_adapter,
        slot_per_adapter,
        layer_input_rows,
        encoded_query_rows,
        encoded_key_rows,
        layer_norm_gain,
        base_value_matrix,
        jnp.swapaxes(adapter_down_panels, 2, 3),
        adapter_up_panels,
    )


def solution(mesh):
    in_specs = (
        P("segment", ("groups", "seq"), None),
        P("segment", ("groups", "seq"), "owner"),
        P("segment", ("groups", "seq"), "owner"),
        P("segment", None),
        P("segment", ("seq", "owner"), None),
        P("segment", "seq", "owner", None),
        P("segment", "seq", None, "owner"),
        P("groups"),
        P("groups"),
        P(),
        P(),
    )
    out_specs = P("segment", ("groups", "seq"), "owner")
    n = mesh.shape["seq"]
    key_heads = KEY_VALUE_HEADS // mesh.shape["owner"]
    small = mesh.shape["owner"] == 2 and n % 2 == 0 and key_heads % n == 0
    return jax.shard_map(
        functools.partial(fused, n) if small else per_device, mesh=mesh, in_specs=in_specs, out_specs=out_specs, check_vma=False
    )
```

```python
import functools

import jax
import jax.numpy as jnp
from jax import lax
from jax.experimental import pallas as pl
from jax.experimental.pallas import tpu as pltpu
from jax.sharding import PartitionSpec as P

WINDOW = 1024
HEADS = 16
KEY_VALUE_HEADS = 8
HEAD_SIZE = 128


query_scale = 168.0 ** (-0.5)
adapter_strength = 32.0
norm_eps = 1e-06


def broadcast(x, axis, root):
    mine = lax.axis_index(axis) == root
    return lax.psum(jnp.where(mine, x, jnp.zeros_like(x)), axis)


def from_behind(value, axis, steps):
    count = lax.axis_size(axis)
    first, last = (max(0, -steps), min(count, count - steps))
    return lax.ppermute(value, axis, [(source, source + steps) for source in range(first, last)])


def per_device(
    layer_input_rows,
    encoded_query_rows,
    encoded_key_rows,
    layer_norm_gain,
    base_value_matrix,
    adapter_down_panels,
    adapter_up_panels,
    request_token_lengths,
    adapter_per_request,
    rank_per_adapter,
    slot_per_adapter,
):
    hidden = layer_input_rows[0]
    row_count = hidden.shape[0]
    seq_now = lax.axis_index("seq")
    owner_now = lax.axis_index("owner")
    reach_count = min(WINDOW // row_count, lax.axis_size("seq") - 1)
    requests = request_token_lengths.shape[0]
    library = slot_per_adapter.shape[0]
    slots_here = adapter_down_panels.shape[1]
    rows_halved = adapter_down_panels.shape[2]
    rank_span_width = adapter_down_panels.shape[3]
    key_value_halved = adapter_up_panels.shape[3]
    group_size = HEADS // KEY_VALUE_HEADS
    request_ends = jnp.cumsum(request_token_lengths)
    position = seq_now * row_count + jnp.arange(row_count, dtype=jnp.int32)
    context = seq_now * row_count + jnp.arange(-reach_count * row_count, row_count, dtype=jnp.int32)
    request_lookup = jnp.sum((position[:, None] >= request_ends[None, :]).astype(jnp.int32), axis=1)
    request_ctx = jnp.sum((context[:, None] >= request_ends[None, :]).astype(jnp.int32), axis=1)
    live_mask = (context[None, :] <= position[:, None]) & (
        context[None, :] > position[:, None] - WINDOW
    )
    live_mask = (
        live_mask & (context[None, :] >= 0) & (request_ctx[None, :] == request_lookup[:, None])
    )
    choose = adapter_per_request[:, None] == jnp.arange(library, dtype=jnp.int32)[None, :]
    slot_of = jnp.sum(jnp.where(choose, slot_per_adapter[None, :], 0), axis=1)
    rank_lookup = jnp.sum(jnp.where(choose, rank_per_adapter[None, :], 0), axis=1)
    scale_lookup = adapter_strength / rank_lookup.astype(jnp.float32)
    in_request = request_lookup[:, None] == jnp.arange(requests, dtype=jnp.int32)[None, :]
    column_live = jnp.arange(rank_span_width, dtype=jnp.int32)[None, :] < rank_lookup[:, None]
    row_gain_weight = jnp.where(in_request, scale_lookup[None, :], jnp.float32(0.0))
    down_panel_here = adapter_down_panels[0]
    up_panel_here = adapter_up_panels[0]
    queries = encoded_query_rows[0]
    keys_own = encoded_key_rows[0]
    key_heads = keys_own.shape[1] // HEAD_SIZE
    wide_rows = hidden.astype(jnp.float32)
    normalized_rows = wide_rows * lax.rsqrt(
        jnp.mean(wide_rows * wide_rows, axis=1, keepdims=True) + norm_eps
    )
    normalized_rows = (normalized_rows * layer_norm_gain[0][None, :]).astype(jnp.bfloat16)
    normed_half = lax.dynamic_slice_in_dim(normalized_rows, owner_now * rows_halved, rows_halved, 1)
    full_value = jnp.dot(
        normalized_rows,
        lax.all_gather(base_value_matrix[0], ("seq", "owner"), axis=0, tiled=True),
        preferred_element_type=jnp.float32,
    )
    value_base_rows = lax.dynamic_slice_in_dim(
        full_value, owner_now * key_value_halved, key_value_halved, 1
    )

    def fetch_one(reduced_rows, request_index):
        owner_slot = slot_of[request_index]
        holder = owner_slot // slots_here
        local_slot = owner_slot % slots_here
        down_local = lax.dynamic_slice_in_dim(down_panel_here, local_slot, 1, 0)
        up_local = lax.dynamic_slice_in_dim(up_panel_here, local_slot, 1, 0)
        down_piece, up_piece = (
            broadcast(down_local, "seq", holder),
            broadcast(up_local, "seq", holder),
        )
        keep_mask = in_request[:, request_index][:, None] & column_live[request_index][None, :]
        matrix_product = jnp.dot(normed_half, down_piece[0], preferred_element_type=jnp.float32)
        return (reduced_rows + jnp.where(keep_mask, matrix_product, jnp.float32(0.0)), up_piece[0])

    start_low = jnp.zeros((row_count, rank_span_width), jnp.float32)
    reduced_rows, panels_up = lax.scan(fetch_one, start_low, jnp.arange(requests, dtype=jnp.int32))
    reduced_rows = lax.psum(reduced_rows, "owner").astype(jnp.bfloat16)
    raised_rows = jnp.einsum(
        "tr,qrk->qtk", reduced_rows, panels_up, preferred_element_type=jnp.float32
    )
    adapter_value = jnp.sum(row_gain_weight.T[:, :, None] * raised_rows, axis=0)
    value_output_rows = (value_base_rows + adapter_value).astype(jnp.bfloat16)
    key_parts = []
    value_parts = []
    for shift_by in range(reach_count, 0, -1):
        key_piece, value_piece = from_behind((keys_own, value_output_rows), "seq", shift_by)
        key_parts.append(key_piece)
        value_parts.append(value_piece)
    keys_all = jnp.concatenate(key_parts + [keys_own], axis=0)
    values_all = jnp.concatenate(value_parts + [value_output_rows], axis=0)
    query_view = queries.reshape(row_count, key_heads, group_size, HEAD_SIZE)
    key_view = keys_all.reshape(-1, key_heads, HEAD_SIZE)
    value_view = values_all.reshape(-1, key_heads, HEAD_SIZE)
    head_outputs = []
    for head_index in range(key_heads):
        query_head = query_view[:, head_index]
        scores = (
            jnp.einsum(
                "tcd,jd->ctj",
                query_head,
                key_view[:, head_index],
                preferred_element_type=jnp.float32,
            )
            * query_scale
        )
        scores = jnp.where(live_mask[None], scores, jnp.float32(-1e30))
        row_max = jnp.max(scores, axis=-1, keepdims=True)
        weights = jnp.exp(scores - row_max)
        row_total = jnp.sum(weights, axis=-1, keepdims=True)
        softmax_rows = (weights / row_total).astype(jnp.bfloat16)
        mixed = jnp.einsum(
            "ctj,jd->tcd",
            softmax_rows,
            value_view[:, head_index],
            preferred_element_type=jnp.float32,
        )
        head_outputs.append(mixed.astype(jnp.bfloat16).reshape(row_count, group_size * HEAD_SIZE))
    result = jnp.concatenate(head_outputs, axis=1)
    return result[None]


ROWS, LANES = 16, 128


def kernel(
    n,
    lengths,
    adapters,
    ranks,
    slots,
    x_hbm,
    q_hbm,
    k_hbm,
    gain_hbm,
    w_hbm,
    down_hbm,
    up_hbm,
    out_hbm,
    xs,
    xf,
    gain,
    wbuf,
    dn,
    dn_guest,
    lp_host,
    base,
    up,
    qb,
    kb,
    lp_mine,
    lp_other,
    part,
    vr,
    prob,
    ob,
    loc_sem,
    x_send_up,
    x_send_dn,
    x_recv,
    f_send,
    f_recv,
    w_send,
    w_recv,
    lp_send,
    lp_recv,
    q_send,
    q_recv,
    k_send,
    k_recv,
    rs_send,
    rs_recv,
    o_send,
    o_recv,
    p_send,
    p_recv,
    hk_send,
):
    f32, bf16 = jnp.float32, jnp.bfloat16
    s = lax.axis_index("seq")
    o = lax.axis_index("owner")
    tok, width = x_hbm.shape[1], x_hbm.shape[2]
    half = width // 2
    win = xf.shape[2]
    slab = w_hbm.shape[1]
    vcols = up.shape[2]
    panel_count, rank_width, _ = dn.shape
    head_cols = vcols // n
    q_cols = qb.shape[2]
    group = HEADS // KEY_VALUE_HEADS
    requests = lengths.shape[0]
    total = n * tok
    chip_rows = width // n
    per_half = n // 2

    def window(of):
        inside = (of % per_half) * chip_rows
        first = min(inside // LANES * LANES, half - win)
        return first, inside - first

    c = s // per_half
    place = lax.rem(s, per_half)
    first, pad = 0, 0
    for step in range(per_half):
        a, b = window(step)
        first = jnp.where(place == step, a, first)
        pad = jnp.where(place == step, b, pad)
    first = pl.multiple_of(first, LANES)
    other = 1 - o
    at_end = (s == 0) | (s == n - 1)
    guest = at_end & (o != c)
    keeper = at_end & (o == c)
    host_low, host_high = (s == 1) & (o == 1), (s == n - 2) & (o == 0)
    host = host_low | host_high
    end_of_host = jnp.where(host_low, 0, n - 1)
    host_seq = jnp.where(s == 0, 1, n - 2)
    can_up = (s < n - 1) & jnp.logical_not(host_high)
    can_down = (s > 0) & jnp.logical_not(host_low)

    def peer(seq, owner=None):
        return {"seq": seq, "owner": o if owner is None else owner}

    def remote(src, dst, send, recv, device):
        return pltpu.make_async_remote_copy(
            src_ref=src,
            dst_ref=dst,
            send_sem=send,
            recv_sem=recv,
            device_id=device,
            device_id_type=pl.DeviceIdType.MESH,
        )

    for step in range(per_half):
        _, b = window(step)

        @pl.when(place == step)
        def _():
            if b:
                wbuf[0:b, :] = jnp.zeros((b, vcols), bf16)
            rest = win - b - chip_rows
            if rest:
                wbuf[win - rest : win, :] = jnp.zeros((rest, vcols), bf16)

    barrier = pltpu.get_barrier_semaphore()
    for d in range(1, n):
        pl.semaphore_signal(
            barrier, inc=1, device_id=peer(lax.rem(s + d, n)), device_id_type=pl.DeviceIdType.MESH
        )
    pl.semaphore_signal(barrier, inc=1, device_id=peer(s, other), device_id_type=pl.DeviceIdType.MESH)

    @pl.when(host)
    def _():
        pl.semaphore_signal(
            barrier, inc=1, device_id=peer(end_of_host, other), device_id_type=pl.DeviceIdType.MESH
        )

    @pl.when(keeper)
    def _():
        pl.semaphore_signal(
            barrier, inc=1, device_id=peer(host_seq, other), device_id_type=pl.DeviceIdType.MESH
        )

    w_at = pl.ds(pl.multiple_of(pad + o * slab, ROWS), slab)
    my_cols = pl.ds(pl.multiple_of(o * vcols, LANES), vcols)
    other_cols = pl.ds(pl.multiple_of(other * vcols, LANES), vcols)
    my_half = pl.ds(pl.multiple_of(o * half, LANES), half)
    x_window = pl.ds(pl.multiple_of(c * half + first, LANES), win)
    my_head = pl.ds(pl.multiple_of(s * head_cols, LANES), head_cols)
    my_q = pl.ds(pl.multiple_of(s * q_cols, LANES), q_cols)
    local = [
        pltpu.make_async_copy(x_hbm.at[0, :, my_half], xs.at[s], loc_sem.at[0]),
        pltpu.make_async_copy(x_hbm.at[0, :, x_window], xf.at[s], loc_sem.at[1]),
        pltpu.make_async_copy(gain_hbm, gain, loc_sem.at[2]),
        pltpu.make_async_copy(down_hbm.at[0], dn, loc_sem.at[3]),
        pltpu.make_async_copy(up_hbm.at[0], up, loc_sem.at[4]),
        pltpu.make_async_copy(w_hbm.at[0, :, my_cols], wbuf.at[w_at], loc_sem.at[5]),
        pltpu.make_async_copy(q_hbm.at[0, :, my_q], qb.at[s], loc_sem.at[6]),
        pltpu.make_async_copy(k_hbm.at[0, :, my_head], kb.at[s], loc_sem.at[7]),
    ]
    for copy in local:
        copy.start()

    pl.semaphore_wait(barrier, n + (host | keeper).astype(jnp.int32))

    def x_copy(t, src, upward):
        to = s + 1 if upward else s - 1
        send = x_send_up if upward else x_send_dn
        return remote(src, xs.at[t], send.at[t], x_recv.at[t], peer(to))

    own_x = x_hbm.at[0, :, my_half]

    @pl.when(can_up)
    def _():
        x_copy(s, own_x, True).start()

    @pl.when(can_down)
    def _():
        x_copy(s, own_x, False).start()

    panel_copy = remote(down_hbm.at[0], dn_guest, p_send, p_recv, peer(host_seq))

    @pl.when(guest)
    def _():
        panel_copy.start()

    w_copy = remote(w_hbm.at[0, :, other_cols], wbuf.at[w_at], w_send, w_recv, peer(s, other))
    w_copy.start()

    def q_copy(to):
        cols = pl.ds(pl.multiple_of(to * q_cols, LANES), q_cols)
        return remote(q_hbm.at[0, :, cols], qb.at[s], q_send.at[to], q_recv.at[s], peer(to))

    def k_copy(to):
        cols = pl.ds(pl.multiple_of(to * head_cols, LANES), head_cols)
        return remote(k_hbm.at[0, :, cols], kb.at[s], k_send.at[to], k_recv.at[s], peer(to))

    ends, slot_of, rank_of = [], [], []
    run = jnp.int32(0)
    for r in range(requests):
        run = run + lengths[r]
        ends.append(run)
        adapter = adapters[r]
        slot_of.append(slots[adapter])
        rank_of.append(ranks[adapter])

    def request_at(position):
        found = jnp.zeros(position.shape, jnp.int32)
        for r in range(requests):
            found = found + (position >= ends[r]).astype(jnp.int32)
        return found

    for at in range(6):
        local[at].wait()

    def f_copy(t):
        return remote(
            xs.at[t, :, pl.ds(first, win)], xf.at[t], f_send.at[t], f_recv.at[t], peer(s, other)
        )

    def lp_copy(t):
        return remote(lp_mine.at[t], lp_other.at[t], lp_send.at[t], lp_recv.at[t], peer(s, other))

    def rs_copy(t, to):
        cols = pl.ds(pl.multiple_of(to * head_cols, LANES), head_cols)
        return remote(part.at[t, :, cols], vr.at[s, t], rs_send.at[t, to], rs_recv.at[s, t], peer(to))

    def host_copies(t):
        return (
            remote(lp_host.at[t], lp_other.at[t], hk_send.at[t], lp_recv.at[t], peer(end_of_host, other)),
        )

    def low_half(t, panels, result):
        rows = xs[t].astype(f32)
        scaled = (rows * gain[:, my_half]).astype(bf16)
        square = jnp.sum(rows * rows, axis=1, keepdims=True)
        product = lax.dot_general(
            scaled,
            panels[...].reshape(panel_count * rank_width, half),
            (((1,), (1,)), ((), ())),
            preferred_element_type=f32,
        )
        result[t, :, : panel_count * rank_width] = product
        result[t, :, panel_count * rank_width :] = jnp.broadcast_to(square, (tok, LANES))

    @pl.when(guest)
    def _():
        lp_mine[...] = jnp.zeros(lp_mine.shape, f32)

    def low_part(t):
        @pl.when(jnp.logical_not(guest))
        def _():
            low_half(t, dn, lp_mine)

        @pl.when(jnp.logical_not(at_end))
        def _():
            lp_copy(t).start()


    def base_part(t):
        scaled = (xf[t].astype(f32) * gain[:, x_window]).astype(bf16)
        base[t] = jnp.dot(scaled, wbuf[...], preferred_element_type=f32)

    def value_part(t):
        lp_copy(t).wait_recv()

        @pl.when(keeper)
        def _():
            lp_host[t] = lp_mine[t] + lp_other[t]
            remote(
                lp_host.at[t], lp_other.at[t], lp_send.at[t], lp_recv.at[t], peer(s, other)
            ).start()

        low_width = panel_count * rank_width
        square = lp_mine[t, :, low_width : low_width + 1] + lp_other[t, :, low_width : low_width + 1]
        inv = lax.rsqrt(square / width + norm_eps)
        low = (lp_mine[t, :, :low_width] + lp_other[t, :, :low_width]) * inv
        req = request_at(t * tok + lax.broadcasted_iota(jnp.int32, (tok, 1), 0))
        slot_t = jnp.zeros((tok, 1), jnp.int32)
        rank_t = jnp.ones((tok, 1), jnp.int32)
        for r in range(requests):
            slot_t = jnp.where(req == r, slot_of[r], slot_t)
            rank_t = jnp.where(req == r, rank_of[r], rank_t)
        column = lax.broadcasted_iota(jnp.int32, (tok, low_width), 1)
        begin = (slot_t - s * panel_count) * rank_width
        low = jnp.where((column >= begin) & (column < begin + rank_t), low, 0.0).astype(bf16)
        raised = jnp.dot(low, up[...].reshape(low_width, vcols), preferred_element_type=f32)
        scale = adapter_strength / rank_t.astype(f32)
        part[t] = (base[t] * inv + raised * scale).astype(bf16)
        for d in range(1, n):
            rs_copy(t, lax.rem(s + d, n)).start()
        vr[s, t] = part[t, :, my_head]

    low_part(s)

    def attention():
        local[6].wait()
        local[7].wait()
        for d in range(1, n):
            frm = lax.rem(s + n - d, n)
            remote(qb.at[frm], qb.at[frm], q_send.at[frm], q_recv.at[frm], peer(frm)).wait_recv()
            remote(kb.at[frm], kb.at[frm], k_send.at[frm], k_recv.at[frm], peer(frm)).wait_recv()
        keys = kb[...].reshape(total, head_cols)
        key_at = lax.broadcasted_iota(jnp.int32, (1, total), 1)
        key_req = request_at(key_at)
        for t in range(n):
            query_at = t * tok + lax.broadcasted_iota(jnp.int32, (tok, 1), 0)
            live = (key_at <= query_at) & (key_at > query_at - WINDOW)
            live = live & (request_at(query_at) == key_req)
            for h in range(q_cols // HEAD_SIZE):
                query = qb[t, :, h * HEAD_SIZE : (h + 1) * HEAD_SIZE]
                kv = h // group
                scores = (
                    lax.dot_general(
                        query,
                        keys[:, kv * HEAD_SIZE : (kv + 1) * HEAD_SIZE],
                        (((1,), (1,)), ((), ())),
                        preferred_element_type=f32,
                    )
                    * query_scale
                )
                scores = jnp.where(live, scores, -1e30)
                weights = jnp.exp(scores - jnp.max(scores, axis=1, keepdims=True))
                soft = weights / jnp.sum(weights, axis=1, keepdims=True)
                prob[h, t * tok : (t + 1) * tok, :] = soft.astype(bf16)

    for d in range(1, n):
        if d == n - 1:

            @pl.when(at_end)
            def _():
                def one(e, carry):
                    value_part(jnp.where(s == 0, e, n - 1 - e))
                    return carry

                lax.fori_loop(0, n - 1, one, 0)

        def arrive(below):
            t = s - d if below else s + d

            @pl.when(((t >= 0) if below else (t < n)) & jnp.logical_not(guest))
            def _():
                x_copy(t, xs.at[t], below).wait_recv()

                @pl.when(can_up if below else can_down)
                def _():
                    x_copy(t, xs.at[t], below).start()

                @pl.when(o == c)
                def _():
                    f_copy(t).start()
                    xf[t] = xs[t, :, pl.ds(first, win)]

        arrive(True)
        arrive(False)

        if d == n - 2:
            for e in range(1, n):
                to = lax.rem(s + e, n)
                q_copy(to).start()
                k_copy(to).start()

        if d == 1:
            w_copy.wait_recv()
            base_part(s)

            @pl.when(jnp.logical_not(at_end))
            def _():
                value_part(s)

        if d == n - 2:

            @pl.when(host)
            def _():
                panel_copy.wait_recv()

                def one(t, carry):
                    low_half(t, dn_guest, lp_host)
                    for copy in host_copies(t):
                        copy.start()
                    return carry

                lax.fori_loop(0, n, one, 0)

        def both(side, carry):
            t = s - d + 2 * d * side

            @pl.when((t >= 0) & (t < n))
            def _():
                low_part(t)

                @pl.when(o != c)
                def _():
                    f_copy(t).wait_recv()

                base_part(t)

                @pl.when(jnp.logical_not(at_end) | (d == n - 1))
                def _():
                    value_part(t)

            return carry

        lax.fori_loop(0, 2, both, 0)

    attention()

    for d in range(1, n):
        frm = lax.rem(s + d, n)
        for t in range(n):
            remote(vr.at[frm, t], vr.at[frm, t], rs_send.at[t, frm], rs_recv.at[frm, t], peer(frm)).wait_recv()
    values = vr[0].astype(f32)
    for frm in range(1, n):
        values = values + vr[frm].astype(f32)
    values = values.reshape(total, head_cols).astype(bf16)

    def o_copy(t):
        return remote(ob.at[t], out_hbm.at[0, :, my_q], o_send.at[t], o_recv.at[s], peer(t))

    for h in range(q_cols // HEAD_SIZE):
        kv = h // group
        mixed = jnp.dot(
            prob[h], values[:, kv * HEAD_SIZE : (kv + 1) * HEAD_SIZE], preferred_element_type=f32
        ).astype(bf16)
        ob[:, :, h * HEAD_SIZE : (h + 1) * HEAD_SIZE] = mixed.reshape(n, tok, HEAD_SIZE)
    for d in range(1, n):
        o_copy(lax.rem(s + d, n)).start()
    mine = pltpu.make_async_copy(ob.at[s], out_hbm.at[0, :, my_q], loc_sem.at[8])
    mine.start()

    w_copy.wait_send()

    @pl.when(guest)
    def _():
        panel_copy.wait_send()

    for d in range(1, n):
        to = lax.rem(s + d, n)
        q_copy(to).wait_send()
        k_copy(to).wait_send()
        for t in range(n):
            rs_copy(t, to).wait_send()
    for t in range(n):

        @pl.when(jnp.logical_not(guest))
        def _():
            lp_copy(t).wait_send()

        @pl.when(host)
        def _():
            for copy in host_copies(t):
                copy.wait_send()

        @pl.when((t <= s) & can_up)
        def _():
            x_copy(t, xs.at[t], True).wait_send()

        @pl.when((t >= s) & can_down)
        def _():
            x_copy(t, xs.at[t], False).wait_send()

        @pl.when((o == c) & (t != s))
        def _():
            f_copy(t).wait_send()

    mine.wait()
    for d in range(1, n):
        frm = lax.rem(s + d, n)
        o_copy(frm).wait_send()
        cols = pl.ds(pl.multiple_of(frm * q_cols, LANES), q_cols)
        remote(ob.at[frm], out_hbm.at[0, :, cols], o_send.at[frm], o_recv.at[frm], peer(frm)).wait_recv()


def fused(
    n,
    layer_input_rows,
    encoded_query_rows,
    encoded_key_rows,
    layer_norm_gain,
    base_value_matrix,
    adapter_down_panels,
    adapter_up_panels,
    request_token_lengths,
    adapter_per_request,
    rank_per_adapter,
    slot_per_adapter,
):
    f32, bf16 = jnp.float32, jnp.bfloat16
    tok, width = layer_input_rows.shape[1:]
    half = width // 2
    panels, _, rank_width = adapter_down_panels.shape[1:]
    vcols = adapter_up_panels.shape[3]
    qcols = encoded_query_rows.shape[2]
    chip_rows = width // n
    pads = [(i * chip_rows) % LANES for i in range(n // 2)]
    win = -(-(max(pads) + chip_rows) // LANES) * LANES
    total = n * tok
    low = panels * rank_width
    dma = pltpu.SemaphoreType.DMA
    any_spec = pl.BlockSpec(memory_space=pl.ANY)
    smem = pl.BlockSpec(memory_space=pltpu.SMEM)
    return pl.pallas_call(
        functools.partial(kernel, n),
        out_shape=jax.ShapeDtypeStruct(encoded_query_rows.shape, bf16),
        in_specs=[smem] * 4 + [any_spec] * 7,
        out_specs=any_spec,
        scratch_shapes=[
            pltpu.VMEM((n, tok, half), bf16),
            pltpu.VMEM((n, tok, win), bf16),
            pltpu.VMEM((1, width), f32),
            pltpu.VMEM((win, vcols), bf16),
            pltpu.VMEM((panels, rank_width, half), bf16),
            pltpu.VMEM((panels, rank_width, half), bf16),
            pltpu.VMEM((n, tok, low + LANES), f32),
            pltpu.VMEM((n, tok, vcols), f32),
            pltpu.VMEM((panels, rank_width, vcols), bf16),
            pltpu.VMEM((n, tok, qcols // n), bf16),
            pltpu.VMEM((n, tok, vcols // n), bf16),
            pltpu.VMEM((n, tok, low + LANES), f32),
            pltpu.VMEM((n, tok, low + LANES), f32),
            pltpu.VMEM((n, tok, vcols), bf16),
            pltpu.VMEM((n, n, tok, vcols // n), bf16),
            pltpu.VMEM((qcols // n // HEAD_SIZE, total, total), bf16),
            pltpu.VMEM((n, tok, qcols // n), bf16),
            dma((9,)),
            dma((n,)),
            dma((n,)),
            dma((n,)),
            dma((n,)),
            dma((n,)),
            dma,
            dma,
            dma((n,)),
            dma((n,)),
            dma((n,)),
            dma((n,)),
            dma((n,)),
            dma((n,)),
            dma((n, n)),
            dma((n, n)),
            dma((n,)),
            dma((n,)),
            dma,
            dma,
            dma((n,)),
        ],
        compiler_params=pltpu.CompilerParams(
            collective_id=0, has_side_effects=True, vmem_limit_bytes=56 * 1024 * 1024
        ),
    )(
        request_token_lengths,
        adapter_per_request,
        rank_per_adapter,
        slot_per_adapter,
        layer_input_rows,
        encoded_query_rows,
        encoded_key_rows,
        layer_norm_gain,
        base_value_matrix,
        jnp.swapaxes(adapter_down_panels, 2, 3),
        adapter_up_panels,
    )


def solution(mesh):
    in_specs = (
        P("segment", ("groups", "seq"), None),
        P("segment", ("groups", "seq"), "owner"),
        P("segment", ("groups", "seq"), "owner"),
        P("segment", None),
        P("segment", ("seq", "owner"), None),
        P("segment", "seq", "owner", None),
        P("segment", "seq", None, "owner"),
        P("groups"),
        P("groups"),
        P(),
        P(),
    )
    out_specs = P("segment", ("groups", "seq"), "owner")
    n = mesh.shape["seq"]
    key_heads = KEY_VALUE_HEADS // mesh.shape["owner"]
    small = mesh.shape["owner"] == 2 and n % 4 == 0 and key_heads % n == 0
    return jax.shard_map(
        functools.partial(fused, n) if small else per_device, mesh=mesh, in_specs=in_specs, out_specs=out_specs, check_vma=False
    )
```
